256 devices in a mesh: section: 32 (over y_hi, z, core), dp: 8 (over y_lo, x).
Axes of the slice: x: 4, y: 4 (y_hi: 2, y_lo: 2; y = y_hi * 2 + y_lo), z: 8, core: 2. Of those that a mesh axis runs over, the one named last changes fastest.
Arguments:
- inputs: bfloat16 [8, 128, 4096], P(None, 'dp'), may hold values from -30 to 30
- in_blocks: bfloat16 [2, 32, 112, 1, 128, 128], P(None, 'section', 'dp'), may hold values from -0.5 to 0.5
- in_ids: int32 [2, 32, 112, 1], P(None, 'section', 'dp'), may hold values from 0 to 31, as said below
- out_blocks: bfloat16 [2, 32, 32, 8, 128, 128], P(None, 'section', 'dp'), may hold values from -0.09375 to 0.09375
- out_ids: int32 [2, 32, 32, 8], P(None, 'section', 'dp'), may hold values from 0 to 111, as said below
Outputs:
- activations: bfloat16 [2, 32, 8, 128, 4096], P(None, 'section', None, 'dp')
The draws below stay inside these ranges and needn't reach their ends.
Inputs may be any that keep to these rules, and one draw needn't show every extreme that they name: `in_ids`: for every layer and every block column, the 1 block rows are distinct. `out_ids`: for every layer and every block column, the 8 block rows are distinct.
All inputs are finite; a program needn't handle non-finite values.
Results may differ from the reference program's by a relative error of at most 0.039.
Values may be sent and summed in bfloat16 or wider, within the bound.
A program may use at most 128 MiB of HBM per device.

```python
import math
import jax
import jax.numpy as jnp
from jax import lax

D = 4096
BLOCK = 128
K_IN = 1
K_OUT = 8
MICRO = 8
SECTIONS = 32
ROWS_ALL = 128
DB = 32
FB = 112


def draw_inputs(key, part):
    base_key = jax.random.fold_in(key, 7)
    key_base, key_cols, key_rows = jax.random.split(base_key, 3)
    shape = (MICRO, ROWS_ALL, D)
    base = jnp.clip(jax.random.normal(key_base, shape, jnp.float32), -6.0, 6.0)
    col_scale = jnp.exp(jax.random.uniform(key_cols, (D,), jnp.float32, 0.0, math.log(10.0)))
    row_scale = jnp.exp(jax.random.uniform(key_rows, (MICRO, ROWS_ALL, 1), jnp.float32, 0.0, math.log(10.0)))
    return (base * col_scale * row_scale / 20.0).astype(jnp.bfloat16)


def distinct_rows(key, count, choose_from, keep):
    keys = jax.random.split(key, count)

    def pick_some(sub_key):
        return jax.random.permutation(sub_key, choose_from)[:keep]
    return jax.vmap(pick_some)(keys).astype(jnp.int32)


def draw_in_ids(key, part):
    chosen = distinct_rows(jax.random.fold_in(key, 11), 2 * SECTIONS * FB, DB, K_IN)
    return chosen.reshape(2, SECTIONS, FB, K_IN)


def draw_out_ids(key, part):
    chosen = distinct_rows(jax.random.fold_in(key, 13), 2 * SECTIONS * DB, FB, K_OUT)
    return chosen.reshape(2, SECTIONS, DB, K_OUT)


def levels(own_key, extent, shards, smallest, high):
    gain, own = 1.0, jax.random.fold_in(own_key, 6)
    for position, shards_of in shards:
        draws = jnp.exp(jax.random.uniform(jax.random.fold_in(own, position), (shards_of,), jnp.float32, smallest / len(shards), high / len(shards)))
        gain = gain * jnp.repeat(draws, extent[position] // shards_of).reshape([-1 if axis == position else 1 for axis in range(len(extent))])
    return gain


def scatter_about(stream_key, shape, width, reach, cuts=(), dtype=jnp.bfloat16):
    values = jax.random.normal(stream_key, shape, jnp.float32) * width
    if len(cuts) > 0:
        values = levels(stream_key, shape, cuts, -0.22, 0.18) * values
    return jnp.clip(values, min=-reach, max=reach).astype(dtype)


def setup_inputs(seed: int = 0) -> dict:
    seeds = jax.random.split(jax.random.key(seed), 6)
    inputs = draw_inputs(jax.random.fold_in(seeds[5], 71), 0)
    in_blocks = scatter_about(seeds[1], (2, SECTIONS, FB, K_IN, BLOCK, BLOCK), (K_IN * BLOCK) ** -0.5, 0.5, ((1, 32), (2, 8)))
    in_ids = draw_in_ids(jax.random.fold_in(seeds[5], 71), 0)
    out_blocks = scatter_about(seeds[3], (2, SECTIONS, DB, K_OUT, BLOCK, BLOCK), (4 * K_OUT * BLOCK) ** -0.5, 0.09375, ((1, 32), (2, 8)))
    out_ids = draw_out_ids(jax.random.fold_in(seeds[5], 71), 0)
    return {"inputs": inputs, "in_blocks": in_blocks, "in_ids": in_ids, "out_blocks": out_blocks, "out_ids": out_ids}


def layer_step(current, layer_args):
    proj_weight, proj_ids, back_weight, back_ids = layer_args
    row_count, feat_count = current.shape
    block_size = proj_weight.shape[-1]
    values = current.astype(jnp.float32)
    inv_root = lax.rsqrt(lax.optimization_barrier(jnp.mean(values * values, axis=-1, keepdims=True)) + 1e-05)
    normed = (values * inv_root).astype(jnp.bfloat16)
    blocks = normed.reshape(row_count, feat_count // block_size, block_size)
    picked = jnp.take(blocks, proj_ids.reshape(-1), axis=1)
    picked = picked.reshape(row_count, proj_ids.shape[0], proj_ids.shape[1], block_size)
    projected = jnp.einsum('rjkc,jkcd->rjd', picked.astype(jnp.float32), proj_weight.astype(jnp.float32))
    hidden = jax.nn.silu(projected).astype(jnp.bfloat16)
    second = jnp.take(hidden, back_ids.reshape(-1), axis=1)
    second = second.reshape(row_count, back_ids.shape[0], back_ids.shape[1], block_size)
    returned = jnp.einsum('rjkc,jkcd->rjd', second.astype(jnp.float32), back_weight.astype(jnp.float32))
    result = (values + returned.reshape(row_count, feat_count)).astype(jnp.bfloat16)
    return (result, result)

def reference(inputs, in_blocks, in_ids, out_blocks, out_ids):
    section_count = in_blocks.shape[1]
    layer_count = 2 * section_count
    micro_count, row_count, feat_count = inputs.shape

    def flatten(array):
        return array.reshape((layer_count,) + array.shape[2:])
    start_rows = inputs.reshape(micro_count * row_count, feat_count)
    final_rows, layer_outs = lax.scan(layer_step, start_rows, (flatten(in_blocks), flatten(in_ids), flatten(out_blocks), flatten(out_ids)))
    return layer_outs.reshape(2, section_count, micro_count, row_count, feat_count)
```

```python
import functools

import jax
import jax.numpy as jnp
from jax import lax
from jax.experimental import pallas as pl
from jax.experimental.pallas import tpu as pltpu
from jax.sharding import PartitionSpec as P

MESH = pl.DeviceIdType.MESH
BLOCK = 128
IN_PER = 14
OUT_PER = 4
K_OUT = 8
PER = IN_PER + OUT_PER * K_OUT
DB = 32
FB = 112
MICRO = 8
ROWS = 16
STAGES = 32
A1, A2, B1, B2 = (0, 11), (11, 10), (21, 13), (34, 12)
A, B = (0, 21), (21, 25)


def layer(x_ref, y_ref, held_ref, hid_ref, w_ref, ids_ref):
    sums = [jnp.zeros((ROWS, BLOCK), jnp.float32) for _ in range(4)]
    for j in range(DB):
        held_ref[j] = x_ref[j]
        v = x_ref[j].astype(jnp.float32)
        sums[j % 4] = sums[j % 4] + v * v
    total = (sums[0] + sums[1]) + (sums[2] + sums[3])
    mean = jnp.sum(total, axis=-1, keepdims=True) * (1.0 / (DB * BLOCK))
    scale = jnp.broadcast_to(lax.rsqrt(mean + 1e-05), (ROWS, BLOCK))
    for j in range(0, FB, 2):
        rows, mats = [], []
        for q in (j, j + 1):
            g, b = q // IN_PER, q % IN_PER
            rows.append(held_ref[ids_ref[g, 0, b]])
            mats.append(w_ref[g, b])
        both = jnp.dot(
            jnp.concatenate(rows, axis=0),
            jnp.concatenate(mats, axis=1),
            preferred_element_type=jnp.float32,
        )
        for q in range(2):
            p = both[q * ROWS : (q + 1) * ROWS, q * BLOCK : (q + 1) * BLOCK] * scale
            hid_ref[j + q] = (p / (1.0 + jnp.exp(-p))).astype(jnp.bfloat16)
    for j in range(DB):
        g, b = j // OUT_PER, IN_PER + (j % OUT_PER) * K_OUT
        picked = jnp.concatenate([hid_ref[ids_ref[g, 0, b + k]] for k in range(K_OUT)], axis=1)
        mat = w_ref[g, pl.ds(b, K_OUT)].reshape(K_OUT * BLOCK, BLOCK)
        back = jnp.dot(picked, mat, preferred_element_type=jnp.float32)
        y_ref[j] = (x_ref[j].astype(jnp.float32) + back).astype(jnp.bfloat16)


def relay(
    x_hbm, in_hbm, out_hbm, ids_hbm, res_hbm,
    w, act, held, hid, ids_vmem, ids_smem,
    load_sem, swap_send, swap_recv, ids_send, ids_recv, ids_local,
    ring_send, ring_recv, hop_send, hop_recv, res_send, res_recv, res_local, go_sem,
):
    section = lax.axis_index("section")
    dp = lax.axis_index("dp")
    m, core = section // 2, section % 2
    other = 1 - core
    x, y = dp % 4, dp // 4
    xr, xl, x2 = (x + 1) % 4, (x + 3) % 4, (x + 2) % 4
    stage = m + 16 * core
    nxt = (stage + 1) % STAGES
    prv = (stage + STAGES - 1) % STAGES
    next_section = 2 * (nxt % 16) + nxt // 16
    prev_section = 2 * (prv % 16) + prv // 16
    twin = (2 * m + other, dp)

    barrier = pltpu.get_barrier_semaphore()
    for d in range(1, 8):
        for c in range(2):
            pl.semaphore_signal(barrier, inc=1, device_id=(2 * m + c, (dp + d) % 8), device_id_type=MESH)
    pl.semaphore_signal(barrier, inc=1, device_id=twin, device_id_type=MESH)
    pl.semaphore_signal(barrier, inc=1, device_id=(next_section, dp), device_id_type=MESH)
    pl.semaphore_signal(barrier, inc=1, device_id=(prev_section, dp), device_id_type=MESH)
    pl.semaphore_wait(barrier, 17)

    mine = [
        pltpu.make_async_copy(in_hbm.at[core], w.at[core, dp, pl.ds(0, IN_PER)], load_sem.at[0]),
        pltpu.make_async_copy(out_hbm.at[core], w.at[core, dp, pl.ds(IN_PER, PER - IN_PER)], load_sem.at[1]),
    ]
    swaps = [
        pltpu.make_async_remote_copy(
            in_hbm.at[other], w.at[core, dp, pl.ds(0, IN_PER)],
            swap_send.at[0], swap_recv.at[0], device_id=twin, device_id_type=MESH),
        pltpu.make_async_remote_copy(
            out_hbm.at[other], w.at[core, dp, pl.ds(IN_PER, PER - IN_PER)],
            swap_send.at[1], swap_recv.at[1], device_id=twin, device_id_type=MESH),
    ]
    for c in mine + swaps:
        c.start()
    landed = [
        pltpu.make_async_remote_copy(
            in_hbm.at[other], w.at[other, dp, pl.ds(0, IN_PER)],
            swap_send.at[0], swap_recv.at[0], device_id=twin, device_id_type=MESH),
        pltpu.make_async_remote_copy(
            out_hbm.at[other], w.at[other, dp, pl.ds(IN_PER, PER - IN_PER)],
            swap_send.at[1], swap_recv.at[1], device_id=twin, device_id_type=MESH),
    ]
    id_own = pltpu.make_async_copy(ids_hbm.at[core], ids_vmem.at[core, dp], ids_local.at[0])
    id_own.start()
    id_copies = []
    for d in range(8):
        peer = (dp + d) % 8
        if d:
            id_copies.append(pltpu.make_async_remote_copy(
                ids_hbm.at[core], ids_vmem.at[core, dp], ids_send.at[2 * d], ids_recv.at[2 * d],
                device_id=(section, peer), device_id_type=MESH))
        id_copies.append(pltpu.make_async_remote_copy(
            ids_hbm.at[other], ids_vmem.at[core, dp], ids_send.at[2 * d + 1], ids_recv.at[2 * d + 1],
            device_id=(2 * m + other, peer), device_id_type=MESH))
    for c in id_copies:
        c.start()
    load_x = pltpu.make_async_copy(x_hbm, act.at[0], load_sem.at[2])

    @pl.when(stage == 0)
    def _():
        load_x.start()

    for c in mine:
        c.wait()
    for c in landed:
        c.wait_recv()

    @pl.when(core == 1)
    def _():
        pl.semaphore_wait(go_sem, 1)

    def at(px, py):
        return py * 4 + px

    to = {
        "r": (section, at(xr, y)),
        "l": (section, at(xl, y)),
        "y": (section, at(x, 1 - y)),
    }
    here, across = at(x, y), at(x, 1 - y)
    plan = [
        ("r", here, A), ("r", here, B), ("r", at(xl, y), A1), ("r", across, B), ("r", at(xl, y), B1), ("r", at(xl, 1 - y), B1),
        ("l", here, A), ("l", here, B), ("l", at(xr, y), A2), ("l", across, B), ("l", at(xr, y), B2), ("l", at(xr, 1 - y), B2),
        ("y", here, B), ("y", here, A), ("y", at(xl, y), A), ("y", at(xr, y), A), ("y", at(x2, y), A1), ("y", at(x2, y), A2),
    ]
    arrive = [
        (at(xl, y), A), (at(xl, y), B), (at(x2, y), A1), (at(xl, 1 - y), B), (at(x2, y), B1), (at(x2, 1 - y), B1),
        (at(xr, y), A), (at(xr, y), B), (at(x2, y), A2), (at(xr, 1 - y), B), (at(x2, y), B2), (at(x2, 1 - y), B2),
        (across, B), (across, A), (at(xl, 1 - y), A), (at(xr, 1 - y), A), (at(x2, 1 - y), A1), (at(x2, 1 - y), A2),
    ]

    def piece(l, t, where):
        g, (first, count) = where
        part = w.at[l, g, pl.ds(first, count)]
        return pltpu.make_async_remote_copy(
            part, part, ring_send.at[l, t], ring_recv.at[l, t], device_id=to[plan[t][0]], device_id_type=MESH)

    def send(l, t):
        piece(l, t, plan[t][1:]).start()

    def got(l, t):
        piece(l, t, arrive[t]).wait_recv()

    for l in range(2):
        for t in (0, 6, 12, 1, 7, 13):
            send(l, t)
    first = [(0, (2, 14)), (6, (8, 15)), (12, (3, 9)), (1, (4,)), (7, (10,)), (13, ())]
    second = [(2, (16,)), (8, (17,)), (3, (5,)), (9, (11,))]
    last = [(t, ()) for t in (4, 10, 14, 15, 5, 11, 16, 17)]
    for group in (first, second, last):
        for l in range(2):
            for t, then in group:
                got(l, t)
                for s in then:
                    send(l, s)
    for l in range(2):
        for t in range(18):
            piece(l, t, plan[t][1:]).wait_send()

    @pl.when(core == 0)
    def _():
        pl.semaphore_signal(go_sem, inc=1, device_id=twin, device_id_type=MESH)

    for c in swaps:
        c.wait_send()
    id_own.wait()
    for d in range(8):
        back = (dp + 8 - d) % 8
        if d:
            pltpu.make_async_remote_copy(
                ids_hbm.at[core], ids_vmem.at[core, back], ids_send.at[2 * d], ids_recv.at[2 * d],
                device_id=(section, back), device_id_type=MESH).wait_recv()
        pltpu.make_async_remote_copy(
            ids_hbm.at[core], ids_vmem.at[other, back], ids_send.at[2 * d + 1], ids_recv.at[2 * d + 1],
            device_id=(2 * m + other, back), device_id_type=MESH).wait_recv()
    for c in id_copies:
        c.wait_send()
    fetch = pltpu.make_async_copy(ids_vmem, ids_smem, ids_local.at[0])
    fetch.start()
    fetch.wait()

    @pl.when(stage == 0)
    def _():
        load_x.wait()

    def hop(i):
        return pltpu.make_async_remote_copy(
            act.at[2, i], act.at[0, i], hop_send.at[i], hop_recv.at[i],
            device_id=(next_section, dp), device_id_type=MESH)

    def result_local(i):
        return pltpu.make_async_copy(act.at[1 + core, i], res_hbm.at[core, i], res_local.at[i])

    def result_remote(i):
        return pltpu.make_async_remote_copy(
            act.at[2 - core, i], res_hbm.at[core, i], res_send.at[i], res_recv.at[i],
            device_id=twin, device_id_type=MESH)

    def result_landed(i):
        return pltpu.make_async_remote_copy(
            act.at[2 - core, i], res_hbm.at[other, i], res_send.at[i], res_recv.at[i],
            device_id=twin, device_id_type=MESH)

    def step(t, carry):
        i, l = t // 2, t % 2

        @pl.when((l == 0) & (stage > 0))
        def _():
            hop(i).wait_recv()

        layer(act.at[l, i], act.at[l + 1, i], held, hid, w.at[l], ids_smem.at[l])

        @pl.when((l == 1) & (stage < STAGES - 1))
        def _():
            hop(i).start()

        @pl.when(l == core)
        def _():
            result_local(i).start()

        @pl.when(l != core)
        def _():
            result_remote(i).start()

        return carry

    lax.fori_loop(0, 2 * MICRO, step, 0)

    def finish(i, carry):
        @pl.when(stage < STAGES - 1)
        def _():
            hop(i).wait_send()

        result_local(i).wait()
        result_remote(i).wait_send()
        result_landed(i).wait_recv()
        return carry

    lax.fori_loop(0, MICRO, finish, 0)


def shards(inputs, in_blocks, in_ids, out_blocks, out_ids):
    x = inputs.reshape(MICRO, ROWS, DB, BLOCK).transpose(0, 2, 1, 3)
    w_in = in_blocks.reshape(2, IN_PER, BLOCK, BLOCK)
    w_out = out_blocks.reshape(2, OUT_PER * K_OUT, BLOCK, BLOCK)
    ids = jnp.concatenate(
        [
            in_ids.reshape(2, 1, IN_PER),
            out_ids.reshape(2, 1, OUT_PER * K_OUT),
            jnp.zeros((2, 1, BLOCK - PER), jnp.int32),
        ],
        axis=2,
    )
    dma = pltpu.SemaphoreType.DMA
    result = pl.pallas_call(
        relay,
        out_shape=jax.ShapeDtypeStruct((2, MICRO, DB, ROWS, BLOCK), jnp.bfloat16),
        in_specs=[pl.BlockSpec(memory_space=pl.ANY)] * 4,
        out_specs=pl.BlockSpec(memory_space=pl.ANY),
        scratch_shapes=[
            pltpu.VMEM((2, 8, PER, BLOCK, BLOCK), jnp.bfloat16),
            pltpu.VMEM((3, MICRO, DB, ROWS, BLOCK), jnp.bfloat16),
            pltpu.VMEM((DB, ROWS, BLOCK), jnp.bfloat16),
            pltpu.VMEM((FB, ROWS, BLOCK), jnp.bfloat16),
            pltpu.VMEM((2, 8, 1, BLOCK), jnp.int32),
            pltpu.SMEM((2, 8, 1, BLOCK), jnp.int32),
            dma((3,)), dma((2,)), dma((2,)), dma((16,)), dma((16,)), dma((1,)),
            dma((2, 18)), dma((2, 18)), dma((MICRO,)), dma((MICRO,)),
            dma((MICRO,)), dma((MICRO,)), dma((MICRO,)),
            pltpu.SemaphoreType.REGULAR,
        ],
        compiler_params=pltpu.CompilerParams(
            collective_id=0, has_side_effects=True, vmem_limit_bytes=60 * 2**20
        ),
    )(x, w_in, w_out, ids)
    result = result.transpose(0, 1, 3, 2, 4).reshape(2, 1, MICRO, ROWS, DB * BLOCK)
    return result


def solution(mesh):
    return jax.shard_map(
        shards,
        mesh=mesh,
        in_specs=(
            P(None, "dp", None),
            P(None, "section", "dp", None, None, None),
            P(None, "section", "dp", None),
            P(None, "section", "dp", None, None, None),
            P(None, "section", "dp", None),
        ),
        out_specs=P(None, "section", None, "dp", None),
        check_vma=False,
    )
```

```python
import functools

import jax
import jax.numpy as jnp
from jax import lax
from jax.experimental import pallas as pl
from jax.experimental.pallas import tpu as pltpu
from jax.sharding import PartitionSpec as P

MESH = pl.DeviceIdType.MESH
BLOCK = 128
IN_PER = 14
OUT_PER = 4
K_OUT = 8
PER = IN_PER + OUT_PER * K_OUT
DB = 32
FB = 112
MICRO = 8
ROWS = 16
STAGES = 32
LAG = 4
PIECE = 4
A1, A2, B1, B2 = (0, 11), (11, 10), (21, 13), (34, 12)
A, B = (0, 21), (21, 25)


def layer(x_ref, y_ref, held_ref, hid_ref, w_ref, ids_ref, emit):
    sums = [jnp.zeros((ROWS, BLOCK), jnp.float32) for _ in range(4)]
    for j in range(DB):
        held_ref[j] = x_ref[j]
        v = x_ref[j].astype(jnp.float32)
        sums[j % 4] = sums[j % 4] + v * v
    total = (sums[0] + sums[1]) + (sums[2] + sums[3])
    mean = jnp.sum(total, axis=-1, keepdims=True) * (1.0 / (DB * BLOCK))
    scale = jnp.broadcast_to(lax.rsqrt(mean + 1e-05), (ROWS, BLOCK))
    for j in range(0, FB, 2):
        rows, mats = [], []
        for q in (j, j + 1):
            g, b = q // IN_PER, q % IN_PER
            rows.append(held_ref[ids_ref[g, 0, b]])
            mats.append(w_ref[g, b])
        both = jnp.dot(
            jnp.concatenate(rows, axis=0),
            jnp.concatenate(mats, axis=1),
            preferred_element_type=jnp.float32,
        )
        for q in range(2):
            p = both[q * ROWS : (q + 1) * ROWS, q * BLOCK : (q + 1) * BLOCK] * scale
            hid_ref[j + q] = (p / (1.0 + jnp.exp(-p))).astype(jnp.bfloat16)
    backs = {}
    for step in range(DB + LAG):
        if step < DB:
            g, b = step // OUT_PER, IN_PER + (step % OUT_PER) * K_OUT
            picked = jnp.concatenate([hid_ref[ids_ref[g, 0, b + k]] for k in range(K_OUT)], axis=1)
            mat = w_ref[g, pl.ds(b, K_OUT)].reshape(K_OUT * BLOCK, BLOCK)
            backs[step] = jnp.dot(picked, mat, preferred_element_type=jnp.float32)
        j = step - LAG
        if j >= 0:
            y_ref[j] = (x_ref[j].astype(jnp.float32) + backs.pop(j)).astype(jnp.bfloat16)
            if emit is not None and (j + 1) % PIECE == 0:
                emit(j + 1 - PIECE)


def relay(
    x_hbm, in_hbm, out_hbm, ids_hbm, res_hbm,
    w, act, held, hid, ids_vmem, ids_smem,
    load_sem, swap_send, swap_recv, ids_send, ids_recv, ids_local,
    ring_send, ring_recv, hop_send, hop_recv, res_send, res_recv, res_local, go_sem,
):
    section = lax.axis_index("section")
    dp = lax.axis_index("dp")
    m, core = section // 2, section % 2
    other = 1 - core
    x, y = dp % 4, dp // 4
    xr, xl, x2 = (x + 1) % 4, (x + 3) % 4, (x + 2) % 4
    stage = m + 16 * core
    nxt = (stage + 1) % STAGES
    prv = (stage + STAGES - 1) % STAGES
    next_section = 2 * (nxt % 16) + nxt // 16
    prev_section = 2 * (prv % 16) + prv // 16
    twin = (2 * m + other, dp)

    barrier = pltpu.get_barrier_semaphore()
    for d in range(1, 8):
        for c in range(2):
            pl.semaphore_signal(barrier, inc=1, device_id=(2 * m + c, (dp + d) % 8), device_id_type=MESH)
    pl.semaphore_signal(barrier, inc=1, device_id=twin, device_id_type=MESH)
    pl.semaphore_signal(barrier, inc=1, device_id=(next_section, dp), device_id_type=MESH)
    pl.semaphore_signal(barrier, inc=1, device_id=(prev_section, dp), device_id_type=MESH)
    pl.semaphore_wait(barrier, 17)

    def at(px, py):
        return py * 4 + px

    here, across = at(x, y), at(x, 1 - y)
    plan = [
        ("r", here, A), ("r", here, B), ("r", at(xl, y), A1), ("r", across, B), ("r", at(xl, y), B1), ("r", at(xl, 1 - y), B1),
        ("l", here, A), ("l", here, B), ("l", at(xr, y), A2), ("l", across, B), ("l", at(xr, y), B2), ("l", at(xr, 1 - y), B2),
        ("y", here, B), ("y", here, A), ("y", at(xl, y), A), ("y", at(xr, y), A), ("y", at(x2, y), A1), ("y", at(x2, y), A2),
    ]
    arrive = [
        (at(xl, y), A), (at(xl, y), B), (at(x2, y), A1), (at(xl, 1 - y), B), (at(x2, y), B1), (at(x2, 1 - y), B1),
        (at(xr, y), A), (at(xr, y), B), (at(x2, y), A2), (at(xr, 1 - y), B), (at(x2, y), B2), (at(x2, 1 - y), B2),
        (across, B), (across, A), (at(xl, 1 - y), A), (at(xr, 1 - y), A), (at(x2, 1 - y), A1), (at(x2, 1 - y), A2),
    ]

    def shard_to(lap, sems):
        return [
            (in_hbm.at[lap], w.at[core, dp, pl.ds(0, IN_PER)]) + tuple(sem.at[0] for sem in sems),
            (out_hbm.at[lap], w.at[core, dp, pl.ds(IN_PER, PER - IN_PER)]) + tuple(sem.at[1] for sem in sems),
        ]

    mine = [pltpu.make_async_copy(*spec) for spec in shard_to(core, (load_sem,))]
    swaps = [
        pltpu.make_async_remote_copy(*spec, device_id=twin, device_id_type=MESH)
        for spec in shard_to(other, (swap_send, swap_recv))
    ]
    landed = [
        pltpu.make_async_remote_copy(
            in_hbm.at[other], w.at[other, dp, pl.ds(0, IN_PER)],
            swap_send.at[0], swap_recv.at[0], device_id=twin, device_id_type=MESH),
        pltpu.make_async_remote_copy(
            out_hbm.at[other], w.at[other, dp, pl.ds(IN_PER, PER - IN_PER)],
            swap_send.at[1], swap_recv.at[1], device_id=twin, device_id_type=MESH),
    ]

    def toward(way, lap):
        px, py = {"r": (xr, y), "l": (xl, y), "y": (x, 1 - y)}[way]
        return (2 * m + lap, at(px, py))

    def send_own(lap):
        slot = jnp.where(lap == core, core, other)
        for t in (0, 6, 12, 1, 7, 13):
            parts = [(out_hbm.at[lap, pl.ds(7, 25)], pl.ds(B[0], B[1]))]
            if plan[t][2] == A:
                parts = [(in_hbm.at[lap], pl.ds(0, IN_PER)), (out_hbm.at[lap, pl.ds(0, 7)], pl.ds(IN_PER, 7))]
            for source, where in parts:
                pltpu.make_async_remote_copy(
                    source, w.at[core, dp, where], ring_send.at[slot, t], ring_recv.at[core, t],
                    device_id=toward(plan[t][0], lap), device_id_type=MESH).start()

    send_own(0)
    for c in mine + swaps:
        c.start()
    id_own = pltpu.make_async_copy(ids_hbm.at[core], ids_vmem.at[core, dp], ids_local.at[0])
    id_own.start()
    id_copies = []
    for d in range(8):
        peer = (dp + d) % 8
        if d:
            id_copies.append(pltpu.make_async_remote_copy(
                ids_hbm.at[core], ids_vmem.at[core, dp], ids_send.at[2 * d], ids_recv.at[2 * d],
                device_id=(section, peer), device_id_type=MESH))
        id_copies.append(pltpu.make_async_remote_copy(
            ids_hbm.at[other], ids_vmem.at[core, dp], ids_send.at[2 * d + 1], ids_recv.at[2 * d + 1],
            device_id=(2 * m + other, peer), device_id_type=MESH))
    for c in id_copies:
        c.start()
    load_x = [
        pltpu.make_async_copy(x_hbm.at[:, h], act.at[0, :, :, pl.ds(8 * h, 8)], load_sem.at[2 + h]) for h in range(2)
    ]

    @pl.when(stage == 0)
    def _():
        for c in load_x:
            c.start()

    @pl.when(core == 1)
    def _():
        pl.semaphore_wait(go_sem, 1)
        send_own(1)

    def piece(l, t, where):
        g, (first, count) = where
        part = w.at[l, g, pl.ds(first, count)]
        return pltpu.make_async_remote_copy(
            part, part, ring_send.at[l, t], ring_recv.at[l, t], device_id=toward(plan[t][0], core), device_id_type=MESH)

    def send(l, t):
        piece(l, t, plan[t][1:]).start()

    def got(l, t):
        piece(l, t, arrive[t]).wait_recv()

    first = [(0, (2, 14)), (6, (8, 15)), (12, (3, 9)), (1, (4,)), (7, (10,)), (13, ())]
    second = [(2, (16,)), (8, (17,)), (3, (5,)), (9, (11,))]
    last = [(t, ()) for t in (4, 10, 14, 15, 5, 11, 16, 17)]
    for group in (first, second, last):
        for l in range(2):
            for t, then in group:
                got(l, t)
                for s in then:
                    send(l, s)

    @pl.when(core == 0)
    def _():
        pl.semaphore_signal(go_sem, inc=1, device_id=twin, device_id_type=MESH)
        send_own(1)

    for c in mine:
        c.wait()
    for c in landed:
        c.wait_recv()
    id_own.wait()
    for d in range(8):
        back = (dp + 8 - d) % 8
        if d:
            pltpu.make_async_remote_copy(
                ids_hbm.at[core], ids_vmem.at[core, back], ids_send.at[2 * d], ids_recv.at[2 * d],
                device_id=(section, back), device_id_type=MESH).wait_recv()
        pltpu.make_async_remote_copy(
            ids_hbm.at[core], ids_vmem.at[other, back], ids_send.at[2 * d + 1], ids_recv.at[2 * d + 1],
            device_id=(2 * m + other, back), device_id_type=MESH).wait_recv()
    for c in id_copies:
        c.wait_send()
    fetch = pltpu.make_async_copy(ids_vmem, ids_smem, ids_local.at[0])
    fetch.start()
    fetch.wait()

    @pl.when(stage == 0)
    def _():
        for c in load_x:
            c.wait()

    def hop(i, spare):
        return pltpu.make_async_remote_copy(
            act.at[2, i], act.at[3 * spare, i], hop_send.at[i], hop_recv.at[spare, i],
            device_id=(next_section, dp), device_id_type=MESH)

    ends = jnp.where(stage == STAGES - 1, 1, 0)
    hop_to = (jnp.where(stage == STAGES - 1, 2 * m + other, next_section), dp)

    def send_hop(i, first):
        part = pl.ds(first, PIECE)
        pltpu.make_async_remote_copy(
            act.at[2, i, part], act.at[3 * ends, i, part], hop_send.at[i], hop_recv.at[ends, i],
            device_id=hop_to, device_id_type=MESH).start()

    def half(l, i, h):
        return act.at[l + 1, i, :, pl.ds(8 * h, 8)]

    def result_local(i, h):
        return pltpu.make_async_copy(half(core, i, h), res_hbm.at[core, i, h], res_local.at[i, h])

    def result_remote(i, h):
        return pltpu.make_async_remote_copy(
            half(other, i, h), res_hbm.at[core, i, h], res_send.at[i, h], res_recv.at[i, h],
            device_id=twin, device_id_type=MESH)

    def result_landed(i, h):
        return pltpu.make_async_remote_copy(
            half(other, i, h), res_hbm.at[other, i, h], res_send.at[i, h], res_recv.at[i, h],
            device_id=twin, device_id_type=MESH)

    def step(i, carry):
        @pl.when(stage > 0)
        def _():
            hop(i, 0).wait_recv()

        layer(act.at[0, i], act.at[1, i], held, hid, w.at[0], ids_smem.at[0], None)
        layer(act.at[1, i], act.at[2, i], held, hid, w.at[1], ids_smem.at[1], functools.partial(send_hop, i))
        for h in range(2):
            result_local(i, h).start()
            result_remote(i, h).start()
        return carry

    lax.fori_loop(0, MICRO, step, 0)

    def finish(i, carry):
        hop(i, 0).wait_send()

        @pl.when(stage == STAGES // 2 - 1)
        def _():
            hop(i, 1).wait_recv()

        for h in range(2):
            result_local(i, h).wait()
            result_remote(i, h).wait_send()
            result_landed(i, h).wait_recv()
        return carry

    for c in swaps:
        c.wait_send()
    for l in range(2):
        for t in range(18):
            piece(l, t, plan[t][1:]).wait_send()
    lax.fori_loop(0, MICRO, finish, 0)


def shards(inputs, in_blocks, in_ids, out_blocks, out_ids):
    x = inputs.reshape(MICRO, 2, 8, DB, BLOCK).transpose(0, 1, 3, 2, 4)
    w_in = in_blocks.reshape(2, IN_PER, BLOCK, BLOCK)
    w_out = out_blocks.reshape(2, OUT_PER * K_OUT, BLOCK, BLOCK)
    ids = jnp.concatenate(
        [
            in_ids.reshape(2, 1, IN_PER),
            out_ids.reshape(2, 1, OUT_PER * K_OUT),
            jnp.zeros((2, 1, BLOCK - PER), jnp.int32),
        ],
        axis=2,
    )
    dma = pltpu.SemaphoreType.DMA
    result = pl.pallas_call(
        relay,
        out_shape=jax.ShapeDtypeStruct((2, MICRO, 2, DB, 8, BLOCK), jnp.bfloat16),
        in_specs=[pl.BlockSpec(memory_space=pl.ANY)] * 4,
        out_specs=pl.BlockSpec(memory_space=pl.ANY),
        scratch_shapes=[
            pltpu.VMEM((2, 8, PER, BLOCK, BLOCK), jnp.bfloat16),
            pltpu.VMEM((4, MICRO, DB, ROWS, BLOCK), jnp.bfloat16),
            pltpu.VMEM((DB, ROWS, BLOCK), jnp.bfloat16),
            pltpu.VMEM((FB, ROWS, BLOCK), jnp.bfloat16),
            pltpu.VMEM((2, 8, 1, BLOCK), jnp.int32),
            pltpu.SMEM((2, 8, 1, BLOCK), jnp.int32),
            dma((4,)), dma((2,)), dma((2,)), dma((16,)), dma((16,)), dma((1,)),
            dma((2, 18)), dma((2, 18)), dma((MICRO,)), dma((2, MICRO)),
            dma((MICRO, 2)), dma((MICRO, 2)), dma((MICRO, 2)),
            pltpu.SemaphoreType.REGULAR,
        ],
        compiler_params=pltpu.CompilerParams(
            collective_id=0, has_side_effects=True, vmem_limit_bytes=60 * 2**20
        ),
    )(x, w_in, w_out, ids)
    result = result.transpose(0, 1, 2, 4, 3, 5).reshape(2, 1, MICRO, ROWS, DB * BLOCK)
    return result


def solution(mesh):
    return jax.shard_map(
        shards,
        mesh=mesh,
        in_specs=(
            P(None, "dp", None),
            P(None, "section", "dp", None, None, None),
            P(None, "section", "dp", None),
            P(None, "section", "dp", None, None, None),
            P(None, "section", "dp", None),
        ),
        out_specs=P(None, "section", None, "dp", None),
        check_vma=False,
    )
```

```python
import functools

import jax
import jax.numpy as jnp
from jax import lax
from jax.experimental import pallas as pl
from jax.experimental.pallas import tpu as pltpu
from jax.sharding import PartitionSpec as P

MESH = pl.DeviceIdType.MESH
BLOCK = 128
IN_PER = 14
OUT_PER = 4
K_OUT = 8
PER = IN_PER + OUT_PER * K_OUT
DB = 32
FB = 112
MICRO = 8
ROWS = 16
STAGES = 32
LAG = 4
PIECE = 4
MAIN = {"A": (0, 17), "A1": (0, 9), "A2": (9, 8), "B": (17, 21), "B1": (17, 11), "B2": (28, 10)}
REST = {"A": (38, 3), "A1": (38, 2), "A2": (40, 1), "B": (41, 5), "B1": (41, 3), "B2": (44, 2)}
REST_AT, REST_LEN = 38, 8
OWN = (0, 6, 12, 1, 7, 13)
FIRST = ((0, (2, 14)), (6, (8, 15)), (12, (3, 9)), (1, (4,)), (7, (10,)), (13, ()))
SECOND = ((2, (16,)), (8, (17,)), (3, (5,)), (9, (11,)))
LAST = tuple((t, ()) for t in (4, 10, 14, 15, 5, 11, 16, 17))
WAYS = "rrrrrrllllllyyyyyy"


def layer(x_ref, y_ref, held_ref, hid_ref, w_ref, ids_ref, emit):
    sums = [jnp.zeros((ROWS, BLOCK), jnp.float32) for _ in range(4)]
    for j in range(DB):
        held_ref[j] = x_ref[j]
        v = x_ref[j].astype(jnp.float32)
        sums[j % 4] = sums[j % 4] + v * v
    total = (sums[0] + sums[1]) + (sums[2] + sums[3])
    mean = jnp.sum(total, axis=-1, keepdims=True) * (1.0 / (DB * BLOCK))
    scale = jnp.broadcast_to(lax.rsqrt(mean + 1e-05), (ROWS, BLOCK))
    for j in range(0, FB, 2):
        rows, mats = [], []
        for q in (j, j + 1):
            g, b = q // IN_PER, q % IN_PER
            rows.append(held_ref[ids_ref[g, 0, b]])
            mats.append(w_ref[g, b])
        both = jnp.dot(
            jnp.concatenate(rows, axis=0),
            jnp.concatenate(mats, axis=1),
            preferred_element_type=jnp.float32,
        )
        for q in range(2):
            p = both[q * ROWS : (q + 1) * ROWS, q * BLOCK : (q + 1) * BLOCK] * scale
            hid_ref[j + q] = (p / (1.0 + jnp.exp(-p))).astype(jnp.bfloat16)
    backs = {}
    for step in range(DB + LAG):
        if step < DB:
            g, b = step // OUT_PER, IN_PER + (step % OUT_PER) * K_OUT
            picked = jnp.concatenate([hid_ref[ids_ref[g, 0, b + k]] for k in range(K_OUT)], axis=1)
            mat = w_ref[g, pl.ds(b, K_OUT)].reshape(K_OUT * BLOCK, BLOCK)
            backs[step] = jnp.dot(picked, mat, preferred_element_type=jnp.float32)
        j = step - LAG
        if j >= 0:
            y_ref[j] = (x_ref[j].astype(jnp.float32) + backs.pop(j)).astype(jnp.bfloat16)
            if emit is not None and (j + 1) % PIECE == 0:
                emit(j + 1 - PIECE)


def relay(
    x_hbm, in_hbm, out_hbm, ids_hbm, res_hbm,
    w, extra, act, held, hid, ids_vmem, ids_smem,
    load_sem, swap_send, swap_recv, ids_send, ids_recv, ids_local,
    ring_send, ring_recv, rest_send, rest_recv, extra_send, extra_recv, feed_send, feed_recv, back_send, back_recv,
    hop_send, hop_recv, res_send, res_recv, res_local, go_sem,
):
    section = lax.axis_index("section")
    dp = lax.axis_index("dp")
    m, core = section // 2, section % 2
    other = 1 - core
    x, y = dp % 4, dp // 4
    xr, xl, x2 = (x + 1) % 4, (x + 3) % 4, (x + 2) % 4
    stage = m + 16 * core
    nxt = (stage + 1) % STAGES
    prv = (stage + STAGES - 1) % STAGES
    next_section = 2 * (nxt % 16) + nxt // 16
    prev_section = 2 * (prv % 16) + prv // 16
    twin = (2 * m + other, dp)
    early = m < 8
    partner = (2 * ((m + 8) % 16) + core, (dp + 4) % 8)
    helped = (core == 0) & early
    helps = (core == 0) & (m >= 8)

    barrier = pltpu.get_barrier_semaphore()
    for d in range(1, 8):
        for c in range(2):
            pl.semaphore_signal(barrier, inc=1, device_id=(2 * m + c, (dp + d) % 8), device_id_type=MESH)
    pl.semaphore_signal(barrier, inc=1, device_id=twin, device_id_type=MESH)
    pl.semaphore_signal(barrier, inc=1, device_id=(next_section, dp), device_id_type=MESH)
    pl.semaphore_signal(barrier, inc=1, device_id=(prev_section, dp), device_id_type=MESH)
    for c in range(2):
        pl.semaphore_signal(barrier, inc=1, device_id=(2 * ((m + 8) % 16) + c, (dp + 4) % 8), device_id_type=MESH)
    pl.semaphore_wait(barrier, 19)

    def at(px, py):
        return py * 4 + px

    def plan_of(parts, row):
        def span(px, flip, name):
            return at(px, 1 - row if flip else row), parts[name]

        sends = [
            span(x, 0, "A"), span(x, 0, "B"), span(xl, 0, "A1"), span(x, 1, "B"), span(xl, 0, "B1"), span(xl, 1, "B1"),
            span(x, 0, "A"), span(x, 0, "B"), span(xr, 0, "A2"), span(x, 1, "B"), span(xr, 0, "B2"), span(xr, 1, "B2"),
            span(x, 0, "B"), span(x, 0, "A"), span(xl, 0, "A"), span(xr, 0, "A"), span(x2, 0, "A1"), span(x2, 0, "A2"),
        ]
        arrivals = [
            span(xl, 0, "A"), span(xl, 0, "B"), span(x2, 0, "A1"), span(xl, 1, "B"), span(x2, 0, "B1"), span(x2, 1, "B1"),
            span(xr, 0, "A"), span(xr, 0, "B"), span(x2, 0, "A2"), span(xr, 1, "B"), span(x2, 0, "B2"), span(x2, 1, "B2"),
            span(x, 1, "B"), span(x, 1, "A"), span(xl, 1, "A"), span(xr, 1, "A"), span(x2, 1, "A1"), span(x2, 1, "A2"),
        ]
        return sends, arrivals

    def shard_to(lap, sems):
        return [
            (in_hbm.at[lap], w.at[core, dp, pl.ds(0, IN_PER)]) + tuple(sem.at[0] for sem in sems),
            (out_hbm.at[lap], w.at[core, dp, pl.ds(IN_PER, PER - IN_PER)]) + tuple(sem.at[1] for sem in sems),
        ]

    mine = [pltpu.make_async_copy(*spec) for spec in shard_to(core, (load_sem,))]
    swaps = [
        pltpu.make_async_remote_copy(*spec, device_id=twin, device_id_type=MESH)
        for spec in shard_to(other, (swap_send, swap_recv))
    ]
    landed = [
        pltpu.make_async_remote_copy(
            in_hbm.at[other], w.at[other, dp, pl.ds(0, IN_PER)],
            swap_send.at[0], swap_recv.at[0], device_id=twin, device_id_type=MESH),
        pltpu.make_async_remote_copy(
            out_hbm.at[other], w.at[other, dp, pl.ds(IN_PER, PER - IN_PER)],
            swap_send.at[1], swap_recv.at[1], device_id=twin, device_id_type=MESH),
    ]

    def toward(way, lap):
        px, py = {"r": (xr, y), "l": (xl, y), "y": (x, 1 - y)}[way]
        return (2 * m + lap, at(px, py))

    def own_copy(lap, way, first, count, send_sem, recv_sem):
        if first == 0:
            sources = [(in_hbm.at[lap], 0, IN_PER), (out_hbm.at[lap, pl.ds(0, count - IN_PER)], IN_PER, count - IN_PER)]
        else:
            sources = [(out_hbm.at[lap, pl.ds(first - IN_PER, count)], first, count)]
        for source, start, length in sources:
            pltpu.make_async_remote_copy(
                source, w.at[core, dp, pl.ds(start, length)], send_sem, recv_sem,
                device_id=toward(way, lap), device_id_type=MESH).start()

    def feed(l):
        return pltpu.make_async_remote_copy(
            out_hbm.at[0, pl.ds(REST_AT - IN_PER, REST_LEN)], extra.at[l, dp], feed_send.at[0], feed_recv.at[l],
            device_id=(2 * ((m + 8) % 16), (dp + 4) % 8), device_id_type=MESH)

    def send_own(lap):
        slot = jnp.where(lap == core, core, other)

        def main():
            for t in OWN:
                first, count = MAIN["A" if t in (0, 6, 13) else "B"]
                own_copy(lap, WAYS[t], first, count, ring_send.at[slot, t], ring_recv.at[core, t])

        def rest():
            for t in OWN:
                first, count = REST["A" if t in (0, 6, 13) else "B"]
                own_copy(lap, WAYS[t], first, count, rest_send.at[slot, t], rest_recv.at[core, t])

        if lap == 1:
            main()
            rest()
        else:
            @pl.when(early)
            def _():
                feed(core).start()

            main()

            @pl.when(m >= 8)
            def _():
                rest()

    @pl.when(early)
    def _():
        send_own(0)

    for c in mine + swaps:
        c.start()
    id_own = pltpu.make_async_copy(ids_hbm.at[core], ids_vmem.at[core, dp], ids_local.at[0])
    id_own.start()
    id_copies = []
    for d in range(8):
        peer = (dp + d) % 8
        if d:
            id_copies.append(pltpu.make_async_remote_copy(
                ids_hbm.at[core], ids_vmem.at[core, dp], ids_send.at[2 * d], ids_recv.at[2 * d],
                device_id=(section, peer), device_id_type=MESH))
        id_copies.append(pltpu.make_async_remote_copy(
            ids_hbm.at[other], ids_vmem.at[core, dp], ids_send.at[2 * d + 1], ids_recv.at[2 * d + 1],
            device_id=(2 * m + other, peer), device_id_type=MESH))
    for c in id_copies:
        c.start()
    load_x = [
        pltpu.make_async_copy(x_hbm.at[:, h], act.at[0, :, :, pl.ds(8 * h, 8)], load_sem.at[2 + h]) for h in range(2)
    ]

    @pl.when(stage == 0)
    def _():
        for c in load_x:
            c.start()

    def relay_over(buf, at_block, parts, row, send_sem, recv_sem):
        sends, arrivals = plan_of(parts, row)

        def piece(l, t, where):
            g, (first, count) = where
            part = buf.at[l, g, pl.ds(first - at_block, count)]
            return pltpu.make_async_remote_copy(
                part, part, send_sem.at[l, t], recv_sem.at[l, t],
                device_id=toward(WAYS[t], core), device_id_type=MESH)

        def start(l, t):
            piece(l, t, sends[t]).start()

        def run(groups, then=None):
            for group in groups:
                for l in range(2):
                    for t, allows in group:
                        piece(l, t, arrivals[t]).wait_recv()
                        for k in allows:
                            start(l, k)
                        if then is not None:
                            then(l, t)

        def sent(l, t):
            piece(l, t, sends[t]).wait_send()

        return start, run, sent, arrivals

    main_start, main_run, main_sent, _ = relay_over(w, 0, MAIN, y, ring_send, ring_recv)
    rest_start, rest_run, rest_sent, rest_arrivals = relay_over(w, 0, REST, y, rest_send, rest_recv)
    extra_start, extra_run, extra_sent, extra_arrivals = relay_over(extra, REST_AT, REST, 1 - y, extra_send, extra_recv)

    def give_back(l, t):
        g, (first, count) = extra_arrivals[t]
        return pltpu.make_async_remote_copy(
            extra.at[l, g, pl.ds(first - REST_AT, count)], w.at[l, g, pl.ds(first, count)],
            back_send.at[l, t], back_recv.at[l, t], device_id=partner, device_id_type=MESH)

    def given_back(l, t):
        g, (first, count) = rest_arrivals[t]
        return pltpu.make_async_remote_copy(
            w.at[l, g, pl.ds(first, count)], w.at[l, g, pl.ds(first, count)],
            back_send.at[l, t], back_recv.at[l, t], device_id=partner, device_id_type=MESH)

    def fed(l):
        client = (dp + 4) % 8
        return pltpu.make_async_remote_copy(
            extra.at[l, client], extra.at[l, client], feed_send.at[0], feed_recv.at[l],
            device_id=partner, device_id_type=MESH)

    def signal_twin():
        pl.semaphore_signal(go_sem, inc=1, device_id=twin, device_id_type=MESH)

    @pl.when(helps)
    def _():
        for l in range(2):
            fed(l).wait_recv()
            for t in OWN:
                extra_start(l, t)
        extra_run((FIRST, SECOND, LAST), lambda l, t: give_back(l, t).start())
        signal_twin()
        send_own(0)

    @pl.when((core == 1) & (m >= 8))
    def _():
        pl.semaphore_wait(go_sem, 1)
        send_own(0)

    @pl.when(core == 1)
    def _():
        pl.semaphore_wait(go_sem, 1)
        send_own(1)

    main_run((FIRST, SECOND, LAST))

    @pl.when(jnp.logical_not(helped))
    def _():
        rest_run((FIRST, SECOND, LAST))

    @pl.when(core == 0)
    def _():
        signal_twin()
        send_own(1)

    @pl.when(helped)
    def _():
        for l in range(2):
            for t in range(18):
                given_back(l, t).wait_recv()

    for c in mine:
        c.wait()
    for c in landed:
        c.wait_recv()
    id_own.wait()
    for d in range(8):
        back = (dp + 8 - d) % 8
        if d:
            pltpu.make_async_remote_copy(
                ids_hbm.at[core], ids_vmem.at[core, back], ids_send.at[2 * d], ids_recv.at[2 * d],
                device_id=(section, back), device_id_type=MESH).wait_recv()
        pltpu.make_async_remote_copy(
            ids_hbm.at[core], ids_vmem.at[other, back], ids_send.at[2 * d + 1], ids_recv.at[2 * d + 1],
            device_id=(2 * m + other, back), device_id_type=MESH).wait_recv()
    for c in id_copies:
        c.wait_send()
    fetch = pltpu.make_async_copy(ids_vmem, ids_smem, ids_local.at[0])
    fetch.start()
    fetch.wait()

    @pl.when(stage == 0)
    def _():
        for c in load_x:
            c.wait()

    def hop(i, spare):
        return pltpu.make_async_remote_copy(
            act.at[2, i], act.at[3 * spare, i], hop_send.at[i], hop_recv.at[spare, i],
            device_id=(next_section, dp), device_id_type=MESH)

    ends = jnp.where(stage == STAGES - 1, 1, 0)
    hop_to = (jnp.where(stage == STAGES - 1, 2 * m + other, next_section), dp)

    def send_hop(i, first):
        part = pl.ds(first, PIECE)
        pltpu.make_async_remote_copy(
            act.at[2, i, part], act.at[3 * ends, i, part], hop_send.at[i], hop_recv.at[ends, i],
            device_id=hop_to, device_id_type=MESH).start()

    def half(l, i, h):
        return act.at[l + 1, i, :, pl.ds(8 * h, 8)]

    def result_local(i, h):
        return pltpu.make_async_copy(half(core, i, h), res_hbm.at[core, i, h], res_local.at[i, h])

    def result_remote(i, h):
        return pltpu.make_async_remote_copy(
            half(other, i, h), res_hbm.at[core, i, h], res_send.at[i, h], res_recv.at[i, h],
            device_id=twin, device_id_type=MESH)

    def result_landed(i, h):
        return pltpu.make_async_remote_copy(
            half(other, i, h), res_hbm.at[other, i, h], res_send.at[i, h], res_recv.at[i, h],
            device_id=twin, device_id_type=MESH)

    def step(i, carry):
        @pl.when(stage > 0)
        def _():
            hop(i, 0).wait_recv()

        layer(act.at[0, i], act.at[1, i], held, hid, w.at[0], ids_smem.at[0], None)
        layer(act.at[1, i], act.at[2, i], held, hid, w.at[1], ids_smem.at[1], functools.partial(send_hop, i))
        for h in range(2):
            result_local(i, h).start()
            result_remote(i, h).start()
        return carry

    lax.fori_loop(0, MICRO, step, 0)

    def finish(i, carry):
        hop(i, 0).wait_send()

        @pl.when(stage == STAGES // 2 - 1)
        def _():
            hop(i, 1).wait_recv()

        for h in range(2):
            result_local(i, h).wait()
            result_remote(i, h).wait_send()
            result_landed(i, h).wait_recv()
        return carry

    for c in swaps:
        c.wait_send()
    for l in range(2):
        for t in range(18):
            main_sent(l, t)

    def rest_own_sent(slot):
        for t in OWN:
            rest_sent(slot, t)

    @pl.when(jnp.logical_not(helped))
    def _():
        rest_own_sent(core)
        for l in range(2):
            for t in range(18):
                if t not in OWN:
                    rest_sent(l, t)

    @pl.when(jnp.logical_not(early & (core == 1)))
    def _():
        rest_own_sent(other)

    @pl.when(early)
    def _():
        feed(core).wait_send()

    @pl.when(helps)
    def _():
        for l in range(2):
            for t in range(18):
                extra_sent(l, t)
                give_back(l, t).wait_send()

    lax.fori_loop(0, MICRO, finish, 0)


def shards(inputs, in_blocks, in_ids, out_blocks, out_ids):
    x = inputs.reshape(MICRO, 2, 8, DB, BLOCK).transpose(0, 1, 3, 2, 4)
    w_in = in_blocks.reshape(2, IN_PER, BLOCK, BLOCK)
    w_out = out_blocks.reshape(2, OUT_PER * K_OUT, BLOCK, BLOCK)
    ids = jnp.concatenate(
        [
            in_ids.reshape(2, 1, IN_PER),
            out_ids.reshape(2, 1, OUT_PER * K_OUT),
            jnp.zeros((2, 1, BLOCK - PER), jnp.int32),
        ],
        axis=2,
    )
    dma = pltpu.SemaphoreType.DMA
    result = pl.pallas_call(
        relay,
        out_shape=jax.ShapeDtypeStruct((2, MICRO, 2, DB, 8, BLOCK), jnp.bfloat16),
        in_specs=[pl.BlockSpec(memory_space=pl.ANY)] * 4,
        out_specs=pl.BlockSpec(memory_space=pl.ANY),
        scratch_shapes=[
            pltpu.VMEM((2, 8, PER, BLOCK, BLOCK), jnp.bfloat16),
            pltpu.VMEM((2, 8, REST_LEN, BLOCK, BLOCK), jnp.bfloat16),
            pltpu.VMEM((4, MICRO, DB, ROWS, BLOCK), jnp.bfloat16),
            pltpu.VMEM((DB, ROWS, BLOCK), jnp.bfloat16),
            pltpu.VMEM((FB, ROWS, BLOCK), jnp.bfloat16),
            pltpu.VMEM((2, 8, 1, BLOCK), jnp.int32),
            pltpu.SMEM((2, 8, 1, BLOCK), jnp.int32),
            dma((4,)), dma((2,)), dma((2,)), dma((16,)), dma((16,)), dma((1,)),
            dma((2, 18)), dma((2, 18)), dma((2, 18)), dma((2, 18)), dma((2, 18)), dma((2, 18)),
            dma((1,)), dma((2,)), dma((2, 18)), dma((2, 18)), dma((MICRO,)), dma((2, MICRO)),
            dma((MICRO, 2)), dma((MICRO, 2)), dma((MICRO, 2)),
            pltpu.SemaphoreType.REGULAR,
        ],
        compiler_params=pltpu.CompilerParams(
            collective_id=0, has_side_effects=True, vmem_limit_bytes=60 * 2**20
        ),
    )(x, w_in, w_out, ids)
    result = result.transpose(0, 1, 2, 4, 3, 5).reshape(2, 1, MICRO, ROWS, DB * BLOCK)
    return result


def solution(mesh):
    return jax.shard_map(
        shards,
        mesh=mesh,
        in_specs=(
            P(None, "dp", None),
            P(None, "section", "dp", None, None, None),
            P(None, "section", "dp", None),
            P(None, "section", "dp", None, None, None),
            P(None, "section", "dp", None),
        ),
        out_specs=P(None, "section", None, "dp", None),
        check_vma=False,
    )
```

```python
import functools

import jax
import jax.numpy as jnp
from jax import lax
from jax.experimental import pallas as pl
from jax.experimental.pallas import tpu as pltpu
from jax.sharding import PartitionSpec as P

MESH = pl.DeviceIdType.MESH
BLOCK = 128
IN_PER = 14
OUT_PER = 4
K_OUT = 8
PER = IN_PER + OUT_PER * K_OUT
DB = 32
FB = 112
MICRO = 8
ROWS = 16
STAGES = 32
LAG = 4
PIECE = 4
MAIN = {"A": (0, 17), "A1": (0, 9), "A2": (9, 8), "B": (17, 21), "B1": (17, 11), "B2": (28, 10)}
REST_AT, REST_LEN = 38, 8
OWN = (0, 6, 12, 1, 7, 13)
FIRST = ((0, (2, 14)), (6, (8, 15)), (12, (3, 9)), (1, (4,)), (7, (10,)), (13, ()))
SECOND = ((2, (16,)), (8, (17,)), (3, (5,)), (9, (11,)))
LAST = tuple((t, ()) for t in (4, 10, 14, 15, 5, 11, 16, 17))
WAYS = "rrrrrrllllllyyyyyy"
MAIN_STEPS = (FIRST, SECOND, LAST)
REST_OWN = (0, 4, 6)
REST_STEPS = (((0, (1,)), (6, (2, 5)), (4, ())), ((2, (3,)),), ((1, ()), (5, ()), (3, ())))
REST_WAYS = "rrrrlly"


def layer(x_ref, y_ref, held_ref, hid_ref, w_ref, in_ref, out_ref, emit):
    sums = [jnp.zeros((ROWS, BLOCK), jnp.float32) for _ in range(4)]
    for j in range(DB):
        held_ref[j] = x_ref[j]
        v = x_ref[j].astype(jnp.float32)
        sums[j % 4] = sums[j % 4] + v * v
    total = (sums[0] + sums[1]) + (sums[2] + sums[3])
    mean = jnp.sum(total, axis=-1, keepdims=True) * (1.0 / (DB * BLOCK))
    scale = jnp.broadcast_to(lax.rsqrt(mean + 1e-05), (ROWS, BLOCK))
    for j in range(0, FB, 2):
        rows, mats = [], []
        for q in (j, j + 1):
            g, b = q // IN_PER, q % IN_PER
            rows.append(held_ref[in_ref[g, 0, b]])
            mats.append(w_ref[g, b])
        both = jnp.dot(
            jnp.concatenate(rows, axis=0),
            jnp.concatenate(mats, axis=1),
            preferred_element_type=jnp.float32,
        )
        for q in range(2):
            p = both[q * ROWS : (q + 1) * ROWS, q * BLOCK : (q + 1) * BLOCK] * scale
            hid_ref[j + q] = (p / (1.0 + jnp.exp(-p))).astype(jnp.bfloat16)
    backs = {}
    for step in range(DB + LAG):
        if step < DB:
            g, b = step // OUT_PER, IN_PER + (step % OUT_PER) * K_OUT
            picked = jnp.concatenate([hid_ref[out_ref[g, step % OUT_PER, k]] for k in range(K_OUT)], axis=1)
            mat = w_ref[g, pl.ds(b, K_OUT)].reshape(K_OUT * BLOCK, BLOCK)
            backs[step] = jnp.dot(picked, mat, preferred_element_type=jnp.float32)
        j = step - LAG
        if j >= 0:
            y_ref[j] = (x_ref[j].astype(jnp.float32) + backs.pop(j)).astype(jnp.bfloat16)
            if emit is not None and (j + 1) % PIECE == 0:
                emit(j + 1 - PIECE)


def relay(
    x_hbm, in_hbm, out_hbm, in_ids, out_ids, res_hbm,
    w, extra, act, held, hid, in_vmem, out_vmem, in_smem, out_smem,
    load_sem, swap_send, swap_recv, ids_send, ids_recv, ids_local,
    ring_send, ring_recv, rest_send, rest_recv, extra_send, extra_recv, feed_send, feed_recv, back_send, back_recv,
    hop_send, hop_recv, res_send, res_recv, res_local, go_sem,
):
    section = lax.axis_index("section")
    dp = lax.axis_index("dp")
    m, core = section // 2, section % 2
    other = 1 - core
    x, y = dp % 4, dp // 4
    xr, xl, x2 = (x + 1) % 4, (x + 3) % 4, (x + 2) % 4
    stage = m + 16 * core
    nxt = (stage + 1) % STAGES
    prv = (stage + STAGES - 1) % STAGES
    next_section = 2 * (nxt % 16) + nxt // 16
    prev_section = 2 * (prv % 16) + prv // 16
    twin = (2 * m + other, dp)
    early = m < 8
    partner = (2 * ((m + 8) % 16) + core, (dp + 4) % 8)
    helped = (core == 0) & early
    helps = (core == 0) & (m >= 8)

    barrier = pltpu.get_barrier_semaphore()
    for d in range(1, 8):
        for c in range(2):
            pl.semaphore_signal(barrier, inc=1, device_id=(2 * m + c, (dp + d) % 8), device_id_type=MESH)
    pl.semaphore_signal(barrier, inc=1, device_id=twin, device_id_type=MESH)
    pl.semaphore_signal(barrier, inc=1, device_id=(next_section, dp), device_id_type=MESH)
    pl.semaphore_signal(barrier, inc=1, device_id=(prev_section, dp), device_id_type=MESH)
    for c in range(2):
        pl.semaphore_signal(barrier, inc=1, device_id=(2 * ((m + 8) % 16) + c, (dp + 4) % 8), device_id_type=MESH)
    pl.semaphore_wait(barrier, 19)

    def at(px, py):
        return py * 4 + px

    def plan_of(parts, row):
        def span(px, flip, name):
            return at(px, 1 - row if flip else row), parts[name]

        sends = [
            span(x, 0, "A"), span(x, 0, "B"), span(xl, 0, "A1"), span(x, 1, "B"), span(xl, 0, "B1"), span(xl, 1, "B1"),
            span(x, 0, "A"), span(x, 0, "B"), span(xr, 0, "A2"), span(x, 1, "B"), span(xr, 0, "B2"), span(xr, 1, "B2"),
            span(x, 0, "B"), span(x, 0, "A"), span(xl, 0, "A"), span(xr, 0, "A"), span(x2, 0, "A1"), span(x2, 0, "A2"),
        ]
        arrivals = [
            span(xl, 0, "A"), span(xl, 0, "B"), span(x2, 0, "A1"), span(xl, 1, "B"), span(x2, 0, "B1"), span(x2, 1, "B1"),
            span(xr, 0, "A"), span(xr, 0, "B"), span(x2, 0, "A2"), span(xr, 1, "B"), span(x2, 0, "B2"), span(x2, 1, "B2"),
            span(x, 1, "B"), span(x, 1, "A"), span(xl, 1, "A"), span(xr, 1, "A"), span(x2, 1, "A1"), span(x2, 1, "A2"),
        ]
        return sends, arrivals

    def rest_plan_of(row):
        part = (REST_AT, REST_LEN)
        far = 1 - row
        sends = [(x, row), (xl, row), (x, far), (xl, far), (x, row), (x, far), (x, row)]
        arrivals = [(xl, row), (x2, row), (xl, far), (x2, far), (xr, row), (xr, far), (x, far)]
        return [(at(*p), part) for p in sends], [(at(*p), part) for p in arrivals]

    def shard_to(lap, sems):
        return [
            (in_hbm.at[lap], w.at[core, dp, pl.ds(0, IN_PER)]) + tuple(sem.at[0] for sem in sems),
            (out_hbm.at[lap], w.at[core, dp, pl.ds(IN_PER, PER - IN_PER)]) + tuple(sem.at[1] for sem in sems),
        ]

    mine = [pltpu.make_async_copy(*spec) for spec in shard_to(core, (load_sem,))]
    swaps = [
        pltpu.make_async_remote_copy(*spec, device_id=twin, device_id_type=MESH)
        for spec in shard_to(other, (swap_send, swap_recv))
    ]
    landed = [
        pltpu.make_async_remote_copy(
            in_hbm.at[other], w.at[other, dp, pl.ds(0, IN_PER)],
            swap_send.at[0], swap_recv.at[0], device_id=twin, device_id_type=MESH),
        pltpu.make_async_remote_copy(
            out_hbm.at[other], w.at[other, dp, pl.ds(IN_PER, PER - IN_PER)],
            swap_send.at[1], swap_recv.at[1], device_id=twin, device_id_type=MESH),
    ]

    def toward(way, lap):
        px, py = {"r": (xr, y), "l": (xl, y), "y": (x, 1 - y)}[way]
        return (2 * m + lap, at(px, py))

    def own_copy(lap, way, first, count, send_sem, recv_sem):
        if first == 0:
            sources = [(in_hbm.at[lap], 0, IN_PER), (out_hbm.at[lap, pl.ds(0, count - IN_PER)], IN_PER, count - IN_PER)]
        else:
            sources = [(out_hbm.at[lap, pl.ds(first - IN_PER, count)], first, count)]
        for source, start, length in sources:
            pltpu.make_async_remote_copy(
                source, w.at[core, dp, pl.ds(start, length)], send_sem, recv_sem,
                device_id=toward(way, lap), device_id_type=MESH).start()

    def feed(l):
        return pltpu.make_async_remote_copy(
            out_hbm.at[0, pl.ds(REST_AT - IN_PER, REST_LEN)], extra.at[l, dp], feed_send.at[0], feed_recv.at[l],
            device_id=(2 * ((m + 8) % 16), (dp + 4) % 8), device_id_type=MESH)

    def send_own(lap):
        slot = jnp.where(lap == core, core, other)

        def main():
            for t in OWN:
                first, count = MAIN["A" if t in (0, 6, 13) else "B"]
                own_copy(lap, WAYS[t], first, count, ring_send.at[slot, t], ring_recv.at[core, t])

        def rest():
            for t in REST_OWN:
                own_copy(lap, REST_WAYS[t], REST_AT, REST_LEN, rest_send.at[slot, t], rest_recv.at[core, t])

        if lap == 1:
            main()
            rest()
        else:
            @pl.when(early)
            def _():
                feed(core).start()

            main()

            @pl.when(m >= 8)
            def _():
                rest()

    @pl.when(early)
    def _():
        send_own(0)

    for c in mine + swaps:
        c.start()
    tables = ((in_ids, in_vmem), (out_ids, out_vmem))

    def id_copy(n, d, c):
        source, table = tables[n]
        return pltpu.make_async_remote_copy(
            source.at[core if c == 0 else other], table.at[core, dp], ids_send.at[n, 2 * d + c], ids_recv.at[n, 2 * d + c],
            device_id=(section if c == 0 else 2 * m + other, (dp + d) % 8), device_id_type=MESH)

    def id_landed(n, d, c):
        source, table = tables[n]
        return pltpu.make_async_remote_copy(
            source.at[core], table.at[core if c == 0 else other, (dp + 8 - d) % 8],
            ids_send.at[n, 2 * d + c], ids_recv.at[n, 2 * d + c],
            device_id=(section if c == 0 else 2 * m + other, (dp + 8 - d) % 8), device_id_type=MESH)

    id_own = [
        pltpu.make_async_copy(source.at[core], table.at[core, dp], ids_local.at[n])
        for n, (source, table) in enumerate(tables)
    ]
    id_pairs = [(n, d, c) for n in range(2) for d in range(8) for c in range(2) if d + c > 0]
    for c in id_own:
        c.start()
    for key in id_pairs:
        id_copy(*key).start()
    load_x = [
        pltpu.make_async_copy(x_hbm.at[:, h], act.at[0, :, :, pl.ds(8 * h, 8)], load_sem.at[2 + h]) for h in range(2)
    ]

    @pl.when(stage == 0)
    def _():
        for c in load_x:
            c.start()

    def relay_over(buf, at_block, plan, ways, send_sem, recv_sem):
        sends, arrivals = plan

        def piece(l, t, where):
            g, (first, count) = where
            part = buf.at[l, g, pl.ds(first - at_block, count)]
            return pltpu.make_async_remote_copy(
                part, part, send_sem.at[l, t], recv_sem.at[l, t],
                device_id=toward(ways[t], core), device_id_type=MESH)

        def start(l, t):
            piece(l, t, sends[t]).start()

        def run(groups, then=None):
            for group in groups:
                for l in range(2):
                    for t, allows in group:
                        piece(l, t, arrivals[t]).wait_recv()
                        for k in allows:
                            start(l, k)
                        if then is not None:
                            then(l, t)

        def sent(l, t):
            piece(l, t, sends[t]).wait_send()

        return start, run, sent, arrivals

    main_start, main_run, main_sent, _ = relay_over(w, 0, plan_of(MAIN, y), WAYS, ring_send, ring_recv)
    rest_start, rest_run, rest_sent, rest_arrivals = relay_over(w, 0, rest_plan_of(y), REST_WAYS, rest_send, rest_recv)
    extra_start, extra_run, extra_sent, extra_arrivals = relay_over(
        extra, REST_AT, rest_plan_of(1 - y), REST_WAYS, extra_send, extra_recv)

    def give_back(l, t):
        g, (first, count) = extra_arrivals[t]
        return pltpu.make_async_remote_copy(
            extra.at[l, g, pl.ds(first - REST_AT, count)], w.at[l, g, pl.ds(first, count)],
            back_send.at[l, t], back_recv.at[l, t], device_id=partner, device_id_type=MESH)

    def given_back(l, t):
        g, (first, count) = rest_arrivals[t]
        return pltpu.make_async_remote_copy(
            w.at[l, g, pl.ds(first, count)], w.at[l, g, pl.ds(first, count)],
            back_send.at[l, t], back_recv.at[l, t], device_id=partner, device_id_type=MESH)

    def fed(l):
        client = (dp + 4) % 8
        return pltpu.make_async_remote_copy(
            extra.at[l, client], extra.at[l, client], feed_send.at[0], feed_recv.at[l],
            device_id=partner, device_id_type=MESH)

    def signal_twin():
        pl.semaphore_signal(go_sem, inc=1, device_id=twin, device_id_type=MESH)

    @pl.when(helps)
    def _():
        for l in range(2):
            fed(l).wait_recv()
            for t in REST_OWN:
                extra_start(l, t)
        extra_run(REST_STEPS, lambda l, t: give_back(l, t).start())
        signal_twin()
        send_own(0)

    @pl.when((core == 1) & (m >= 8))
    def _():
        pl.semaphore_wait(go_sem, 1)
        send_own(0)

    @pl.when(core == 1)
    def _():
        pl.semaphore_wait(go_sem, 1)
        send_own(1)

    main_run(MAIN_STEPS)

    @pl.when(jnp.logical_not(helped))
    def _():
        rest_run(REST_STEPS)

    @pl.when(core == 0)
    def _():
        signal_twin()
        send_own(1)

    @pl.when(helped)
    def _():
        for l in range(2):
            for t in range(7):
                given_back(l, t).wait_recv()

    for c in mine:
        c.wait()
    for c in landed:
        c.wait_recv()
    for c in id_own:
        c.wait()
    for key in id_pairs:
        id_landed(*key).wait_recv()
    fetch = [
        pltpu.make_async_copy(in_vmem, in_smem, ids_local.at[0]),
        pltpu.make_async_copy(out_vmem, out_smem, ids_local.at[1]),
    ]
    for c in fetch:
        c.start()
    for c in fetch:
        c.wait()

    @pl.when(stage == 0)
    def _():
        for c in load_x:
            c.wait()

    def hop(i, spare):
        return pltpu.make_async_remote_copy(
            act.at[2, i], act.at[3 * spare, i], hop_send.at[i], hop_recv.at[spare, i],
            device_id=(next_section, dp), device_id_type=MESH)

    ends = jnp.where(stage == STAGES - 1, 1, 0)
    hop_to = (jnp.where(stage == STAGES - 1, 2 * m + other, next_section), dp)

    def send_hop(i, first):
        part = pl.ds(first, PIECE)
        pltpu.make_async_remote_copy(
            act.at[2, i, part], act.at[3 * ends, i, part], hop_send.at[i], hop_recv.at[ends, i],
            device_id=hop_to, device_id_type=MESH).start()

    def half(l, i, h):
        return act.at[l + 1, i, :, pl.ds(8 * h, 8)]

    def result_local(i, h):
        return pltpu.make_async_copy(half(core, i, h), res_hbm.at[core, i, h], res_local.at[i, h])

    def result_remote(i, h):
        return pltpu.make_async_remote_copy(
            half(other, i, h), res_hbm.at[core, i, h], res_send.at[i, h], res_recv.at[i, h],
            device_id=twin, device_id_type=MESH)

    def result_landed(i, h):
        return pltpu.make_async_remote_copy(
            half(other, i, h), res_hbm.at[other, i, h], res_send.at[i, h], res_recv.at[i, h],
            device_id=twin, device_id_type=MESH)

    def step(i, carry):
        @pl.when(stage > 0)
        def _():
            hop(i, 0).wait_recv()

        layer(act.at[0, i], act.at[1, i], held, hid, w.at[0], in_smem.at[0], out_smem.at[0], None)
        layer(act.at[1, i], act.at[2, i], held, hid, w.at[1], in_smem.at[1], out_smem.at[1], functools.partial(send_hop, i))
        for h in range(2):
            result_local(i, h).start()
            result_remote(i, h).start()
        return carry

    lax.fori_loop(0, MICRO, step, 0)

    def finish(i, carry):
        hop(i, 0).wait_send()

        @pl.when(stage == STAGES // 2 - 1)
        def _():
            hop(i, 1).wait_recv()

        for h in range(2):
            result_local(i, h).wait()
            result_remote(i, h).wait_send()
            result_landed(i, h).wait_recv()
        return carry

    for c in swaps:
        c.wait_send()
    for key in id_pairs:
        id_copy(*key).wait_send()
    for l in range(2):
        for t in range(18):
            main_sent(l, t)

    def rest_own_sent(slot):
        for t in REST_OWN:
            rest_sent(slot, t)

    @pl.when(jnp.logical_not(helped))
    def _():
        rest_own_sent(core)
        for l in range(2):
            for t in (1, 2, 3, 5):
                rest_sent(l, t)

    @pl.when(jnp.logical_not(early & (core == 1)))
    def _():
        rest_own_sent(other)

    @pl.when(early)
    def _():
        feed(core).wait_send()

    @pl.when(helps)
    def _():
        for l in range(2):
            for t in range(7):
                extra_sent(l, t)
                give_back(l, t).wait_send()

    lax.fori_loop(0, MICRO, finish, 0)


def shards(inputs, in_blocks, in_ids, out_blocks, out_ids):
    x = inputs.reshape(MICRO, 2, 8, DB, BLOCK).transpose(0, 1, 3, 2, 4)
    w_in = in_blocks.reshape(2, IN_PER, BLOCK, BLOCK)
    w_out = out_blocks.reshape(2, OUT_PER * K_OUT, BLOCK, BLOCK)
    dma = pltpu.SemaphoreType.DMA
    result = pl.pallas_call(
        relay,
        out_shape=jax.ShapeDtypeStruct((2, MICRO, 2, DB, 8, BLOCK), jnp.bfloat16),
        in_specs=[pl.BlockSpec(memory_space=pl.ANY)] * 5,
        out_specs=pl.BlockSpec(memory_space=pl.ANY),
        scratch_shapes=[
            pltpu.VMEM((2, 8, PER, BLOCK, BLOCK), jnp.bfloat16),
            pltpu.VMEM((2, 8, REST_LEN, BLOCK, BLOCK), jnp.bfloat16),
            pltpu.VMEM((4, MICRO, DB, ROWS, BLOCK), jnp.bfloat16),
            pltpu.VMEM((DB, ROWS, BLOCK), jnp.bfloat16),
            pltpu.VMEM((FB, ROWS, BLOCK), jnp.bfloat16),
            pltpu.VMEM((2, 8, 1, IN_PER), jnp.int32),
            pltpu.VMEM((2, 8, OUT_PER, K_OUT), jnp.int32),
            pltpu.SMEM((2, 8, 1, IN_PER), jnp.int32),
            pltpu.SMEM((2, 8, OUT_PER, K_OUT), jnp.int32),
            dma((4,)), dma((2,)), dma((2,)), dma((2, 16)), dma((2, 16)), dma((2,)),
            dma((2, 18)), dma((2, 18)), dma((2, 7)), dma((2, 7)), dma((2, 7)), dma((2, 7)),
            dma((1,)), dma((2,)), dma((2, 7)), dma((2, 7)), dma((MICRO,)), dma((2, MICRO)),
            dma((MICRO, 2)), dma((MICRO, 2)), dma((MICRO, 2)),
            pltpu.SemaphoreType.REGULAR,
        ],
        compiler_params=pltpu.CompilerParams(
            collective_id=0, has_side_effects=True, vmem_limit_bytes=60 * 2**20
        ),
    )(x, w_in, w_out, in_ids.reshape(2, 1, IN_PER), out_ids.reshape(2, OUT_PER, K_OUT))
    result = result.transpose(0, 1, 2, 4, 3, 5).reshape(2, 1, MICRO, ROWS, DB * BLOCK)
    return result


def solution(mesh):
    return jax.shard_map(
        shards,
        mesh=mesh,
        in_specs=(
            P(None, "dp", None),
            P(None, "section", "dp", None, None, None),
            P(None, "section", "dp", None),
            P(None, "section", "dp", None, None, None),
            P(None, "section", "dp", None),
        ),
        out_specs=P(None, "section", None, "dp", None),
        check_vma=False,
    )
```
